256 devices in a mesh: seq: 8 (over z), head: 4 (over y_hi, core), rep: 8 (over y_lo, x).
Axes of the slice: x: 4, y: 4 (y_hi: 2, y_lo: 2; y = y_hi * 2 + y_lo), z: 8, core: 2. Of those that a mesh axis runs over, the one named last changes fastest.
Arguments:
- queries: bfloat16 [8, 2048, 7168], P('rep', 'seq', 'head'), may hold values from -6 to 6
- new_keys: bfloat16 [8, 2048, 7168], P('rep', 'seq', 'head'), may hold values from -6 to 6
- new_values: bfloat16 [8, 2048, 7168], P('rep', 'seq', 'head'), may hold values from -4 to 4
- lengths: int32 [8, 4], P('rep'), may hold values from 1 to 1024, 2048 in all within a row
- offsets: int32 [8, 4], P('rep'), may hold values from 0 to 4095
- slot_map: int32 [8, 4], P('rep'), may hold values from 0 to 3, each once within a row
Outputs:
- attended: bfloat16 [8, 2048, 7168], P('rep', 'seq', 'head')
- key_cache: bfloat16 [8, 4, 1024, 7168], P('rep', 'head', None, 'seq')
- value_cache: bfloat16 [8, 4, 1024, 7168], P('rep', 'head', None, 'seq')
The draws below stay inside these ranges and needn't reach their ends.
Inputs may be any that keep to these rules, and one draw needn't show every extreme that they name: `lengths`: each row sums to 2048; its first entry is the group's shared prompt; every row has one entry equal to 1024. `slot_map`: each row is a permutation of the group's requests.
All inputs are finite; a program needn't handle non-finite values.
Results may differ from the reference program's by a relative error of at most 0.011.
Values may be sent and summed in bfloat16 or wider, within the bound.
A program may use at most 128 MiB of HBM per device.

```python
import math
import jax
import jax.numpy as jnp
import numpy as np
from jax import lax

HEADS = 32
HD = 224
GROUPS = 8
TOKENS = 2048
REQS = 4
LMAX = 1024


def draw_queries(key, part):
    shape_all = (GROUPS, TOKENS, HEADS * HD)
    return jnp.clip(jax.random.normal(jax.random.fold_in(key, 11), shape_all, jnp.float32), -4.0, 4.0).astype(jnp.bfloat16)


def draw_new_keys(key, part):
    shape_all = (GROUPS, TOKENS, HEADS * HD)
    return jnp.clip(jax.random.normal(jax.random.fold_in(key, 12), shape_all, jnp.float32), -4.0, 4.0).astype(jnp.bfloat16)


def place_ends(entries, key, low, top_value):
    longest = entries.shape.index(max(entries.shape))
    spots = []
    for shift in (0, 1):
        where = [jax.random.randint(jax.random.fold_in(key, axis), (), 0, length) for axis, length in enumerate(entries.shape)]
        where[longest] = (where[longest] + shift) % entries.shape[longest]
        spots.append(tuple(where))
    return entries.at[spots[0]].set(low).at[spots[1]].set(top_value)


def block_levels(key, dims, pieces, smallest, high):
    gain = 1.0
    for dim, shards_of in pieces:
        heights = jax.random.uniform(jax.random.fold_in(jax.random.fold_in(key, 6), dim), (shards_of,), jnp.float32, smallest / len(pieces), high / len(pieces))
        gain = gain * jnp.repeat(jnp.exp(heights), dims[dim] // shards_of).reshape((-1,) + (1,) * (len(dims) - 1 - dim))
    return gain


def split_up(number_of, total, limit, slope):
    portions = [(1 << 20) // math.isqrt(standing ** slope) + 1 for standing in range(2, number_of + 1)]
    surplus, given = total - limit - (number_of - 1), [1] * (number_of - 1)
    while surplus > 0:
        movable = [i for i in range(number_of - 1) if given[i] < limit]
        pool, remaining = sum([portions[i] for i in movable]), surplus
        for i in movable:
            extra = min(limit - given[i], max(1, remaining * portions[i] // pool), surplus)
            given[i] = given[i] + extra
            surplus = surplus - extra
    return np.array([limit] + given)


def ragged_sizes(rng, number_of, total, bound, skew):
    if number_of == 2:
        one = jax.random.randint(rng, (), max(1, total - bound), min(bound, total - 1) + 1)
        return jnp.stack([one, total - one])
    sizes = jnp.asarray(split_up(number_of, total, bound, skew), jnp.int32)
    pairs = (number_of - 1) // 2
    donor, receiver = sizes[1:1 + 2 * pairs:2], sizes[2:2 + 2 * pairs:2]
    room = jnp.minimum(donor - 1, bound - receiver)
    moved = jax.random.randint(jax.random.fold_in(rng, 1), (pairs,), 0, 1 << 20) % (room + 1)
    sizes = sizes.at[1:1 + 2 * pairs:2].set(donor - moved).at[2:2 + 2 * pairs:2].set(receiver + moved)
    return sizes[jax.random.permutation(jax.random.fold_in(rng, 2), number_of)]


def normal_values(key, extent, width, bound, cuts=(), kind=jnp.bfloat16):
    values = width * jax.random.normal(key, extent, jnp.float32)
    if cuts:
        values = values * block_levels(key, extent, cuts, -0.22, 0.18)
    return jnp.clip(values, -bound, bound).astype(kind)


def setup_inputs(seed: int = 0) -> dict:
    splits = jax.random.split(jax.random.key(seed), 7)
    return {
        "queries": draw_queries(jax.random.fold_in(splits[6], 71), 0),
        "new_keys": draw_new_keys(jax.random.fold_in(splits[6], 71), 0),
        "new_values": normal_values(splits[2], (GROUPS, TOKENS, HEADS * HD), 1.0, 4.0, ((0, 8), (1, 8), (2, 4))),
        "lengths": jax.vmap(lambda own: ragged_sizes(own, REQS, TOKENS, LMAX, 2))(jax.random.split(splits[3], GROUPS)).reshape((GROUPS, REQS)).astype(jnp.int32),
        "offsets": place_ends(jax.random.randint(splits[4], (GROUPS, REQS), 0, 4096), jax.random.fold_in(splits[4], 1), 0, 4095).astype(jnp.int32),
        "slot_map": jax.vmap(lambda own: jax.random.permutation(own, REQS))(jax.random.split(splits[5], GROUPS)).reshape((GROUPS, REQS)).astype(jnp.int32),
    }


NEG_FILL = -1e+30
ROPE_BASE = 10000.0

def rotate(source, places):
    full_width = source.shape[-1]
    half_width = full_width // 2
    inverse = jnp.power(jnp.float32(ROPE_BASE), -2.0 * jnp.arange(half_width, dtype=jnp.float32) / full_width)
    angles = places.astype(jnp.float32)[:, None] * inverse[None, :]
    cosine = jnp.cos(angles)[:, None, :]
    sine_terms = jnp.sin(angles)[:, None, :]
    first_part = source[..., :half_width].astype(jnp.float32)
    second_part = source[..., half_width:].astype(jnp.float32)
    rotated = jnp.concatenate([first_part * cosine - second_part * sine_terms, second_part * cosine + first_part * sine_terms], axis=-1)
    return rotated.astype(jnp.bfloat16)

def group_outputs(operands):
    query_token_rows, key_rows, value_rows, lengths_row, offsets_row, slots_row = operands
    ends_at = jnp.cumsum(lengths_row).astype(jnp.int32)
    begins = (ends_at - lengths_row).astype(jnp.int32)
    token_ids = jnp.arange(TOKENS, dtype=jnp.int32)
    request = lax.optimization_barrier(jnp.sum((token_ids[:, None] >= ends_at[None, :]).astype(jnp.int32), axis=1)).astype(jnp.int32)
    places = (offsets_row[request] + token_ids - begins[request]).astype(jnp.int32)
    rot_queries = rotate(query_token_rows.reshape(TOKENS, HEADS, HD), places)
    rot_keys = rotate(key_rows.reshape(TOKENS, HEADS, HD), places)
    value_heads = value_rows.reshape(TOKENS, HEADS, HD)
    same_request = (request[None, :] == request[:, None]) & (token_ids[None, :] <= token_ids[:, None])
    prompt_keys = (request[None, :] == 0) & (request[:, None] != 0)
    allowed = same_request | prompt_keys

    def one_head(head_operands):
        single_query_head, key_head, value_head = head_operands
        scores = jnp.dot(single_query_head, key_head.T, preferred_element_type=jnp.float32) * (1.0 / math.sqrt(HD))
        scores = jnp.where(allowed, scores, NEG_FILL)
        row_max = lax.optimization_barrier(jnp.max(scores, axis=1, keepdims=True))
        expons = jnp.where(allowed, jnp.exp(scores - row_max), 0.0)
        row_total = lax.optimization_barrier(jnp.sum(expons, axis=1, keepdims=True))
        mixed = jnp.dot(expons.astype(jnp.bfloat16), value_head, preferred_element_type=jnp.float32)
        return (mixed / row_total).astype(jnp.bfloat16)
    per_head_outputs = lax.map(one_head, (rot_queries.transpose(1, 0, 2), rot_keys.transpose(1, 0, 2), value_heads.transpose(1, 0, 2)))
    attended_rows = per_head_outputs.transpose(1, 0, 2).reshape(TOKENS, HEADS * HD)
    flat_keys = rot_keys.reshape(TOKENS, HEADS * HD)
    filler = jnp.zeros((LMAX, HEADS * HD), jnp.bfloat16)
    padded_keys = jnp.concatenate([flat_keys, filler], axis=0)
    padded_values = jnp.concatenate([value_rows, filler], axis=0)
    slot_index = jnp.arange(LMAX, dtype=jnp.int32)
    key_pieces = []
    value_pieces = []
    for number in range(REQS):
        keep_rows = (slot_index < lengths_row[number])[:, None]
        begin_at = begins[number].astype(jnp.int32)
        key_pieces.append(jnp.where(keep_rows, lax.dynamic_slice_in_dim(padded_keys, begin_at, LMAX, 0), jnp.zeros((), jnp.bfloat16)))
        value_pieces.append(jnp.where(keep_rows, lax.dynamic_slice_in_dim(padded_values, begin_at, LMAX, 0), jnp.zeros((), jnp.bfloat16)))
    key_slots = jnp.zeros((REQS, LMAX, HEADS * HD), jnp.bfloat16).at[slots_row].set(jnp.stack(key_pieces))
    value_slots = jnp.zeros((REQS, LMAX, HEADS * HD), jnp.bfloat16).at[slots_row].set(jnp.stack(value_pieces))
    return (attended_rows, key_slots, value_slots)

def reference(queries, new_keys, new_values, lengths, offsets, slot_map):
    attended, key_cache, value_cache = lax.map(group_outputs, (queries, new_keys, new_values, lengths, offsets, slot_map))
    return (attended, key_cache, value_cache)
```

```python
import functools
import math

import jax
import jax.numpy as jnp
from jax import lax
from jax.experimental import pallas as pl
from jax.experimental.pallas import tpu as pltpu
from jax.sharding import PartitionSpec as P

HD = 224
HALF = HD // 2
ROPE_BASE = 10000.0
NEG_FILL = -1e30
MESH = pl.DeviceIdType.MESH
VMEM = pltpu.VMEM
STEPS = (4, 3, -3, 2, -2, 1, -1)
V, K, Q = 0, 1, 2


def rotate_kernel(v_ref, k_ref, q_ref, cos_ref, sin_ref, out_ref):
    cos, sin = cos_ref[...], sin_ref[...]
    for t, ref in ((V, v_ref), (K, k_ref), (Q, q_ref)):
        flipped = ref[...].T
        for i in range(4):
            if t == V:
                out_ref[t, i, 0] = flipped[i * HD : (i + 1) * HD]
            else:
                a = flipped[i * HD : i * HD + HALF].astype(jnp.float32)
                b = flipped[i * HD + HALF : (i + 1) * HD].astype(jnp.float32)
                out_ref[t, i, 0, :HALF] = (a * cos - b * sin).astype(jnp.bfloat16)
                out_ref[t, i, 0, HALF:] = (b * cos + a * sin).astype(jnp.bfloat16)


def rotated_blocks(queries, keys, values, cos, sin):
    tok = queries.shape[0]
    wide = pl.BlockSpec((tok, 4 * HD), lambda e: (0, e))
    table = pl.BlockSpec((HALF, tok), lambda e: (0, 0))
    return pl.pallas_call(
        rotate_kernel,
        grid=(2,),
        out_shape=jax.ShapeDtypeStruct((3, 4, 2, HD, tok), jnp.bfloat16),
        in_specs=[wide, wide, wide, table, table],
        out_specs=pl.BlockSpec((3, 4, 1, HD, tok), lambda e: (0, 0, e, 0, 0)),
        compiler_params=pltpu.CompilerParams(vmem_limit_bytes=48 << 20),
        name="rotate",
    )(values, keys, queries, cos, sin)


def exchange_kernel(
    x_ref, begin_ref, prompt_ref, kv_ref, out_ref,
    mid, rec, kn, osend,
    in_s, in_r, z_s, z_r, y_s, y_r, c_s, c_r, f_s, f_r, own_s, o_s, o_r,
):
    s, h, r = lax.axis_index("seq"), lax.axis_index("head"), lax.axis_index("rep")
    tok = rec.shape[-1]
    core, high = h % 2, h // 2
    c1 = high * 2 + (1 - core)
    y1 = (1 - high) * 2 + core
    y2 = (1 - high) * 2 + (1 - core)
    partners = (h, c1, y1, y2)
    o_self = s // 2 == h

    def remote(src, dst, send, recv, seq, head):
        return pltpu.make_async_remote_copy(
            src_ref=src, dst_ref=dst, send_sem=send, recv_sem=recv,
            device_id=(seq, head, r), device_id_type=MESH,
        )

    bar = pltpu.get_barrier_semaphore()
    for p in partners[1:]:
        pl.semaphore_signal(bar, inc=1, device_id=(s, p, r), device_id_type=MESH)
    for d in range(1, 8):
        pl.semaphore_signal(bar, inc=1, device_id=((s + d) % 8, h, r), device_id_type=MESH)
    for e in range(2):
        for p in range(4):
            here = (2 * h + e == s) & (p == h)

            @pl.when(jnp.logical_not(here))
            def _():
                pl.semaphore_signal(bar, inc=1, device_id=(2 * h + e, p, r), device_id_type=MESH)

    @pl.when(o_self)
    def _():
        pl.semaphore_wait(bar, 17)

    @pl.when(jnp.logical_not(o_self))
    def _():
        pl.semaphore_wait(bar, 18)

    def plane(t, rel, e):
        return remote(
            x_ref.at[t, partners[rel], e], mid.at[t, rel, e],
            in_s.at[t, rel, e], in_r.at[t, rel, e], s, partners[rel],
        )

    def plane_own(t, e):
        return pltpu.make_async_copy(x_ref.at[t, h, e], mid.at[t, 0, e], in_r.at[t, 0, e])

    for t in (V, K, Q):
        for e in range(2):
            plane(t, 2, e).start()
            plane(t, 3, e).start()
        for e in range(2):
            plane_own(t, e).start()
            plane(t, 1, e).start()

    def z_place(to):
        hs, e = to // 2, to % 2
        rel = (h % 2 + hs % 2) % 2 + 2 * ((h // 2 + hs // 2) % 2)
        return rel, e

    def z_issue(t):
        for n, d in enumerate(STEPS):
            to = (s + d + 8) % 8
            rel, e = z_place(to)
            pltpu.make_async_copy(mid.at[t, rel, e], mid.at[t, rel, e], in_r.at[t, rel, e]).wait()
            remote(mid.at[t, rel, e], rec.at[t, s], z_s.at[t, n], z_r.at[t, n], to, h).start()
        rel, e = z_place(s)
        pltpu.make_async_copy(mid.at[t, rel, e], mid.at[t, rel, e], in_r.at[t, rel, e]).wait()
        pltpu.make_async_copy(mid.at[t, rel, e], rec.at[t, s], z_r.at[t, 7]).start()

    def z_from(n):
        return s if n == 7 else (s - STEPS[n] + 8) % 8

    def z_wait(t, n):
        blk = z_from(n)
        pltpu.make_async_copy(rec.at[t, blk], rec.at[t, blk], z_r.at[t, n]).wait()
        return blk

    def share(t, n, blk):
        return (
            remote(rec.at[t, blk], kv_ref.at[t, blk, h], y_s.at[t, n], y_r.at[t, n], s, y1),
            remote(rec.at[t, blk], kv_ref.at[t, blk, h], c_s.at[t, n], c_r.at[t, n], s, c1),
            pltpu.make_async_copy(rec.at[t, blk], kv_ref.at[t, blk, h], own_s.at[t, n]),
        )

    def pass_on(t, n):
        blk = z_from(n)
        return remote(
            kv_ref.at[t, blk, y1], kv_ref.at[t, blk, y1], f_s.at[t, n], f_r.at[t, n], s, c1
        )

    def pass_wait(t, n):
        share(t, n, z_from(n))[0].wait_recv()
        pass_on(t, n).start()

    z_issue(V)
    z_issue(K)
    for n in (7, 0, 1, 2, 3, 4, 5, 6):
        blk = z_wait(V, n)
        for copy in share(V, n, blk):
            copy.start()
    z_issue(Q)
    for n in (7, 0, 1, 2, 3, 4, 5, 6):
        blk = z_wait(K, n)
        for copy in share(K, n, blk):
            copy.start()
        kn[blk] = rec[K, blk].T

    key_rel = lax.broadcasted_iota(jnp.int32, (tok, tok), 0)
    query_rel = lax.broadcasted_iota(jnp.int32, (tok, tok), 1)
    rate = math.log2(math.e) / math.sqrt(HD)
    prompt = prompt_ref[...]

    def attend(blk):
        q = rec[Q, blk]
        first = begin_ref[blk]

        def scores(j):
            raw = jnp.dot(kn[j], q, preferred_element_type=jnp.float32)
            place = key_rel + j * tok
            return raw, (place < prompt) | (place >= first)

        raw, seen = scores(blk)
        sc = jnp.where(seen & (key_rel <= query_rel), raw, NEG_FILL)
        best = jnp.max(sc, axis=0, keepdims=True)
        w = jnp.exp2((sc - best) * rate)
        total = jnp.sum(w, axis=0, keepdims=True)
        acc = jnp.dot(rec[V, blk], w.astype(jnp.bfloat16), preferred_element_type=jnp.float32)

        def step(j, state):
            best, total, acc = state
            raw, seen = scores(j)
            sc = jnp.where(seen, raw, NEG_FILL)
            new = jnp.maximum(best, jnp.max(sc, axis=0, keepdims=True))
            keep = jnp.exp2((best - new) * rate)
            w = jnp.exp2((sc - new) * rate)
            total = total * keep + jnp.sum(w, axis=0, keepdims=True)
            acc = acc * keep + jnp.dot(
                rec[V, j], w.astype(jnp.bfloat16), preferred_element_type=jnp.float32
            )
            return new, total, acc

        best, total, acc = lax.fori_loop(0, blk, step, (best, total, acc))
        osend[blk] = (acc / total).astype(jnp.bfloat16)

    mine = (s % 2) * 4 + h

    def give(blk, n):
        return remote(osend.at[blk], out_ref.at[mine], o_s.at[n], o_r.at[mine], blk, s // 2)

    def give_own():
        return pltpu.make_async_copy(osend.at[s], out_ref.at[mine], o_r.at[mine])

    for n in range(8):
        blk = z_wait(Q, n)
        attend(blk)
        if n < 7:
            give(blk, n).start()
        else:

            @pl.when(o_self)
            def _():
                give_own().start()

            @pl.when(jnp.logical_not(o_self))
            def _():
                give(blk, 7).start()

        pass_wait(V, (7, 0, 1, 2, 3, 4, 5, 6)[n])
    for n in (7, 0, 1, 2, 3, 4, 5, 6):
        pass_wait(K, n)

    for j in range(8):
        pltpu.make_async_copy(out_ref.at[j], out_ref.at[j], o_r.at[j]).wait()
    for t in (V, K):
        for n in range(8):
            yc, cc, oc = share(t, n, z_from(n))
            oc.wait()
            yc.wait_send()
            cc.wait()
            pass_on(t, n).wait()
    for t in (V, K, Q):
        for e in range(2):
            for rel in (1, 2, 3):
                plane(t, rel, e).wait_send()
        for n in range(7):
            remote(rec.at[t, s], rec.at[t, s], z_s.at[t, n], z_r.at[t, n], s, c1).wait_send()
    for n in range(7):
        give(z_from(n), n).wait_send()

    @pl.when(jnp.logical_not(o_self))
    def _():
        give(s, 7).wait_send()


def exchange(blocks, begin_rows, prompt_row):
    tok = blocks.shape[-1]
    seq = 2048 // tok
    dma = pltpu.SemaphoreType.DMA
    block = (HD, tok)
    return pl.pallas_call(
        exchange_kernel,
        out_shape=(
            jax.ShapeDtypeStruct((2, seq, 4) + block, jnp.bfloat16),
            jax.ShapeDtypeStruct((8,) + block, jnp.bfloat16),
        ),
        in_specs=[
            pl.BlockSpec(memory_space=pl.ANY),
            pl.BlockSpec(memory_space=VMEM),
            pl.BlockSpec(memory_space=VMEM),
        ],
        out_specs=(pl.BlockSpec(memory_space=pl.ANY), pl.BlockSpec(memory_space=pl.ANY)),
        scratch_shapes=[
            VMEM((3, 4, 2) + block, jnp.bfloat16),
            VMEM((3, seq) + block, jnp.bfloat16),
            VMEM((seq, tok, HD), jnp.bfloat16),
            VMEM((seq,) + block, jnp.bfloat16),
            dma((3, 4, 2)), dma((3, 4, 2)),
            dma((3, 8)), dma((3, 8)),
            dma((2, 8)), dma((2, 8)),
            dma((2, 8)), dma((2, 8)),
            dma((2, 8)), dma((2, 8)),
            dma((2, 8)),
            dma((8,)), dma((8,)),
        ],
        compiler_params=pltpu.CompilerParams(
            collective_id=0, has_side_effects=True, vmem_limit_bytes=56 << 20
        ),
        name="exchange",
    )(blocks, begin_rows, prompt_row)


def window_kernel(info_ref, lo_ref, hi_ref, cache_ref):
    p = pl.program_id(1)
    tok = lo_ref.shape[-1]
    shift, length = info_ref[1], info_ref[2]
    row = lax.broadcasted_iota(jnp.int32, (tok, tok), 0)
    col = lax.broadcasted_iota(jnp.int32, (tok, tok), 1)
    kept = row + p * tok < length
    low = jnp.where(kept & (col == row + shift), 1.0, 0.0).astype(jnp.bfloat16)
    high = jnp.where(kept & (col + tok == row + shift), 1.0, 0.0).astype(jnp.bfloat16)
    dims = (((1,), (1,)), ((), ()))
    cut = lax.dot_general(low, lo_ref[0, 0], dims, preferred_element_type=jnp.float32)
    cut += lax.dot_general(high, hi_ref[0, 0], dims, preferred_element_type=jnp.float32)
    cache_ref[0] = cut.astype(jnp.bfloat16)


def windows(info, kv):
    _, seq, rows, tok = kv.shape
    steps = seq // 2

    def low(t, p, info):
        return (t, jnp.minimum(info[0] + p, seq - 1), 0, 0)

    def high(t, p, info):
        return (t, jnp.minimum(info[0] + p + 1, seq - 1), 0, 0)

    return pl.pallas_call(
        window_kernel,
        grid_spec=pltpu.PrefetchScalarGridSpec(
            num_scalar_prefetch=1,
            grid=(2, steps),
            in_specs=[pl.BlockSpec((1, 1, rows, tok), low), pl.BlockSpec((1, 1, rows, tok), high)],
            out_specs=pl.BlockSpec((1, tok, rows), lambda t, p, info: (t, p, 0)),
        ),
        out_shape=jax.ShapeDtypeStruct((2, steps * tok, rows), jnp.bfloat16),
        name="windows",
    )(info, kv, kv)


def flip_kernel(x_ref, o_ref):
    o_ref[...] = x_ref[...].T


def flip(x):
    rows, tok = x.shape
    return pl.pallas_call(
        flip_kernel,
        grid=(2,),
        out_shape=jax.ShapeDtypeStruct((tok, rows), x.dtype),
        in_specs=[pl.BlockSpec((rows // 2, tok), lambda i: (i, 0))],
        out_specs=pl.BlockSpec((tok, rows // 2), lambda i: (0, i)),
        name="flip",
    )(x)


def per_device(queries, new_keys, new_values, lengths, offsets, slot_map):
    tok = queries.shape[1]
    seq = lax.axis_size("seq")
    lengths_row, offsets_row, slots_row = lengths[0], offsets[0], slot_map[0]
    ends = jnp.cumsum(lengths_row)
    begins = ends - lengths_row
    tokens = jnp.arange(tok * seq, dtype=jnp.int32)
    request = jnp.sum((tokens[:, None] >= ends[None, :]).astype(jnp.int32), axis=1)
    pick = request[:, None] == jnp.arange(4, dtype=jnp.int32)[None, :]
    begin_of = jnp.sum(jnp.where(pick, begins[None, :], 0), axis=1)
    place = jnp.sum(jnp.where(pick, (offsets_row - begins)[None, :], 0), axis=1) + tokens
    mine = lax.dynamic_slice_in_dim(place, lax.axis_index("seq") * tok, tok, 0)
    inverse = jnp.power(
        jnp.float32(ROPE_BASE), -2.0 * jnp.arange(HALF, dtype=jnp.float32) / HD
    )
    angles = inverse[:, None] * mine.astype(jnp.float32)[None, :]
    blocks = rotated_blocks(
        queries[0], new_keys[0], new_values[0], jnp.cos(angles), jnp.sin(angles)
    )
    begin_rows = begin_of.reshape(seq, 1, tok)
    prompt_row = jnp.broadcast_to(lengths_row[0], (1, tok))
    kv, attended = exchange(blocks, begin_rows, prompt_row)
    owner = slots_row == lax.axis_index("head")
    begin = jnp.sum(jnp.where(owner, begins, 0))
    length = jnp.sum(jnp.where(owner, lengths_row, 0))
    info = jnp.stack([begin // tok, begin % tok, length])
    caches = windows(info, kv.reshape(2, seq, 4 * HD, tok))
    return (flip(attended.reshape(8 * HD, tok))[None], caches[1][None, None], caches[0][None, None])


def solution(mesh):
    full = P("rep", "seq", "head")
    row = P("rep", None)
    cache = P("rep", "head", None, "seq")
    return jax.shard_map(
        per_device, mesh=mesh, in_specs=(full, full, full, row, row, row),
        out_specs=(full, cache, cache), check_vma=False,
    )
```

```python
import functools
import math

import jax
import jax.numpy as jnp
from jax import lax
from jax.experimental import pallas as pl
from jax.experimental.pallas import tpu as pltpu
from jax.sharding import PartitionSpec as P

HD = 224
HALF = HD // 2
ROPE_BASE = 10000.0
NEG_FILL = -1e30
MESH = pl.DeviceIdType.MESH
VMEM = pltpu.VMEM
STEPS = (4, 3, -3, 2, -2, 1, -1)
V, K, Q = 0, 1, 2
EXCHANGE_VMEM = 28 << 20
FINISH_VMEM = 28 << 20


def rotate_kernel(lens_ref, offs_ref, v_ref, k_ref, q_ref, rate_ref, out_ref, cos_ref, sin_ref):
    @pl.when(pl.program_id(0) == 0)
    def _():
        tok = cos_ref.shape[-1]
        token = lax.broadcasted_iota(jnp.int32, (1, tok), 1) + lax.axis_index("seq") * tok
        ahead = jnp.full((1, tok), offs_ref[0, 0], jnp.int32)
        end = lens_ref[0, 0]
        for r in range(1, 4):
            ahead = jnp.where(token >= end, offs_ref[0, r] - end, ahead)
            end += lens_ref[0, r]
        angles = rate_ref[...] * (token + ahead).astype(jnp.float32)
        cos_ref[...] = jnp.cos(angles)
        sin_ref[...] = jnp.sin(angles)

    cos, sin = cos_ref[...], sin_ref[...]
    for t, ref in ((V, v_ref), (K, k_ref), (Q, q_ref)):
        flipped = ref[...].T
        for i in range(4):
            if t == V:
                out_ref[t, i, 0] = flipped[i * HD : (i + 1) * HD]
            else:
                a = flipped[i * HD : i * HD + HALF].astype(jnp.float32)
                b = flipped[i * HD + HALF : (i + 1) * HD].astype(jnp.float32)
                out_ref[t, i, 0, :HALF] = (a * cos - b * sin).astype(jnp.bfloat16)
                out_ref[t, i, 0, HALF:] = (b * cos + a * sin).astype(jnp.bfloat16)


def rotated_blocks(lengths, offsets, queries, keys, values, rates):
    tok = queries.shape[0]
    wide = pl.BlockSpec((tok, 4 * HD), lambda e: (0, e))
    scalars = pl.BlockSpec(memory_space=pltpu.SMEM)
    return pl.pallas_call(
        rotate_kernel,
        grid=(2,),
        out_shape=jax.ShapeDtypeStruct((3, 4, 2, HD, tok), jnp.bfloat16),
        in_specs=[
            scalars, scalars, wide, wide, wide, pl.BlockSpec((HALF, 1), lambda e: (0, 0)),
        ],
        out_specs=pl.BlockSpec((3, 4, 1, HD, tok), lambda e: (0, 0, e, 0, 0)),
        scratch_shapes=[VMEM((HALF, tok), jnp.float32), VMEM((HALF, tok), jnp.float32)],
        compiler_params=pltpu.CompilerParams(vmem_limit_bytes=48 << 20),
        name="rotate",
    )(lengths, offsets, values, keys, queries, rates)


def exchange_kernel(
    x_ref, lens_ref, kv_ref, out_ref,
    mid, rec, kn, osend,
    in_s, in_r, z_s, z_r, y_s, y_r, c_s, c_r, f_s, f_r, own_s, o_s, o_r,
):
    s, h, r = lax.axis_index("seq"), lax.axis_index("head"), lax.axis_index("rep")
    tok = rec.shape[-1]
    core, high = h % 2, h // 2
    c1 = high * 2 + (1 - core)
    y1 = (1 - high) * 2 + core
    y2 = (1 - high) * 2 + (1 - core)
    partners = (h, c1, y1, y2)
    o_self = s // 2 == h

    def remote(src, dst, send, recv, seq, head):
        return pltpu.make_async_remote_copy(
            src_ref=src, dst_ref=dst, send_sem=send, recv_sem=recv,
            device_id=(seq, head, r), device_id_type=MESH,
        )

    bar = pltpu.get_barrier_semaphore()
    for p in partners[1:]:
        pl.semaphore_signal(bar, inc=1, device_id=(s, p, r), device_id_type=MESH)
    for d in range(1, 8):
        pl.semaphore_signal(bar, inc=1, device_id=((s + d) % 8, h, r), device_id_type=MESH)
    for e in range(2):
        for p in range(4):
            here = (2 * h + e == s) & (p == h)

            @pl.when(jnp.logical_not(here))
            def _():
                pl.semaphore_signal(bar, inc=1, device_id=(2 * h + e, p, r), device_id_type=MESH)

    @pl.when(o_self)
    def _():
        pl.semaphore_wait(bar, 17)

    @pl.when(jnp.logical_not(o_self))
    def _():
        pl.semaphore_wait(bar, 18)

    def plane(t, rel, e):
        return remote(
            x_ref.at[t, partners[rel], e], mid.at[t, rel, e],
            in_s.at[t, rel, e], in_r.at[t, rel, e], s, partners[rel],
        )

    def plane_own(t, e):
        return pltpu.make_async_copy(x_ref.at[t, h, e], mid.at[t, 0, e], in_r.at[t, 0, e])

    for t in (V, K, Q):
        for e in range(2):
            plane(t, 2, e).start()
            plane(t, 3, e).start()
        for e in range(2):
            plane_own(t, e).start()
            plane(t, 1, e).start()

    def z_place(to):
        hs, e = to // 2, to % 2
        rel = (h % 2 + hs % 2) % 2 + 2 * ((h // 2 + hs // 2) % 2)
        return rel, e

    def z_issue(t):
        for n, d in enumerate(STEPS):
            to = (s + d + 8) % 8
            rel, e = z_place(to)
            pltpu.make_async_copy(mid.at[t, rel, e], mid.at[t, rel, e], in_r.at[t, rel, e]).wait()
            remote(mid.at[t, rel, e], rec.at[t, s], z_s.at[t, n], z_r.at[t, n], to, h).start()
        rel, e = z_place(s)
        pltpu.make_async_copy(mid.at[t, rel, e], mid.at[t, rel, e], in_r.at[t, rel, e]).wait()
        pltpu.make_async_copy(mid.at[t, rel, e], rec.at[t, s], z_r.at[t, 7]).start()

    def z_from(n):
        return s if n == 7 else (s - STEPS[n] + 8) % 8

    def z_wait(t, n):
        blk = z_from(n)
        pltpu.make_async_copy(rec.at[t, blk], rec.at[t, blk], z_r.at[t, n]).wait()
        return blk

    def share(t, n, blk):
        return (
            remote(rec.at[t, blk], kv_ref.at[t, blk, h], y_s.at[t, n], y_r.at[t, n], s, y1),
            remote(rec.at[t, blk], kv_ref.at[t, blk, h], c_s.at[t, n], c_r.at[t, n], s, c1),
            pltpu.make_async_copy(rec.at[t, blk], kv_ref.at[t, blk, h], own_s.at[t, n]),
        )

    def pass_on(t, n):
        blk = z_from(n)
        return remote(
            kv_ref.at[t, blk, y1], kv_ref.at[t, blk, y1], f_s.at[t, n], f_r.at[t, n], s, c1
        )

    def pass_wait(t, n):
        share(t, n, z_from(n))[0].wait_recv()
        pass_on(t, n).start()

    z_issue(V)
    z_issue(K)
    for n in (7, 0, 1, 2, 3, 4, 5, 6):
        blk = z_wait(V, n)
        for copy in share(V, n, blk):
            copy.start()
    z_issue(Q)
    for n in (7, 0, 1, 2, 3, 4, 5, 6):
        blk = z_wait(K, n)
        for copy in share(K, n, blk):
            copy.start()
        kn[blk] = rec[K, blk].T

    key_rel = lax.broadcasted_iota(jnp.int32, (tok, tok), 0)
    query_rel = lax.broadcasted_iota(jnp.int32, (tok, tok), 1)
    rate = math.log2(math.e) / math.sqrt(HD)
    prompt = lens_ref[0, 0]
    token_rel = lax.broadcasted_iota(jnp.int32, (1, tok), 1)

    def attend(blk):
        q = rec[Q, blk]
        token = token_rel + blk * tok
        first = jnp.zeros_like(token)
        end = 0
        for r in range(3):
            end += lens_ref[0, r]
            first = jnp.where(token >= end, end, first)

        def scores(j):
            raw = jnp.dot(kn[j], q, preferred_element_type=jnp.float32)
            place = key_rel + j * tok
            return raw, (place < prompt) | (place >= first)

        raw, seen = scores(blk)
        sc = jnp.where(seen & (key_rel <= query_rel), raw, NEG_FILL)
        best = jnp.max(sc, axis=0, keepdims=True)
        w = jnp.exp2((sc - best) * rate)
        total = jnp.sum(w, axis=0, keepdims=True)
        acc = jnp.dot(rec[V, blk], w.astype(jnp.bfloat16), preferred_element_type=jnp.float32)

        def step(j, state):
            best, total, acc = state
            raw, seen = scores(j)
            sc = jnp.where(seen, raw, NEG_FILL)
            new = jnp.maximum(best, jnp.max(sc, axis=0, keepdims=True))
            keep = jnp.exp2((best - new) * rate)
            w = jnp.exp2((sc - new) * rate)
            total = total * keep + jnp.sum(w, axis=0, keepdims=True)
            acc = acc * keep + jnp.dot(
                rec[V, j], w.astype(jnp.bfloat16), preferred_element_type=jnp.float32
            )
            return new, total, acc

        best, total, acc = lax.fori_loop(0, blk, step, (best, total, acc))
        osend[blk] = (acc / total).astype(jnp.bfloat16)

    mine = (s % 2) * 4 + h

    def give(blk, n):
        return remote(osend.at[blk], out_ref.at[mine], o_s.at[n], o_r.at[mine], blk, s // 2)

    def give_own():
        return pltpu.make_async_copy(osend.at[s], out_ref.at[mine], o_r.at[mine])

    for n in range(8):
        blk = z_wait(Q, n)
        attend(blk)
        if n < 7:
            give(blk, n).start()
        else:

            @pl.when(o_self)
            def _():
                give_own().start()

            @pl.when(jnp.logical_not(o_self))
            def _():
                give(blk, 7).start()

        pass_wait(V, (7, 0, 1, 2, 3, 4, 5, 6)[n])
    for n in (7, 0, 1, 2, 3, 4, 5, 6):
        pass_wait(K, n)

    for j in range(8):
        pltpu.make_async_copy(out_ref.at[j], out_ref.at[j], o_r.at[j]).wait()
    for t in (V, K):
        for n in range(8):
            yc, cc, oc = share(t, n, z_from(n))
            oc.wait()
            yc.wait_send()
            cc.wait()
            pass_on(t, n).wait()
    for t in (V, K, Q):
        for e in range(2):
            for rel in (1, 2, 3):
                plane(t, rel, e).wait_send()
        for n in range(7):
            remote(rec.at[t, s], rec.at[t, s], z_s.at[t, n], z_r.at[t, n], s, c1).wait_send()
    for n in range(7):
        give(z_from(n), n).wait_send()

    @pl.when(jnp.logical_not(o_self))
    def _():
        give(s, 7).wait_send()


def exchange(blocks, lengths):
    tok = blocks.shape[-1]
    seq = 2048 // tok
    dma = pltpu.SemaphoreType.DMA
    block = (HD, tok)
    return pl.pallas_call(
        exchange_kernel,
        out_shape=(
            jax.ShapeDtypeStruct((2, seq, 4) + block, jnp.bfloat16),
            jax.ShapeDtypeStruct((8,) + block, jnp.bfloat16),
        ),
        in_specs=[
            pl.BlockSpec(memory_space=pl.ANY),
            pl.BlockSpec(memory_space=pltpu.SMEM),
        ],
        out_specs=(pl.BlockSpec(memory_space=pl.ANY), pl.BlockSpec(memory_space=pl.ANY)),
        scratch_shapes=[
            VMEM((3, 4, 2) + block, jnp.bfloat16),
            VMEM((3, seq) + block, jnp.bfloat16),
            VMEM((seq, tok, HD), jnp.bfloat16),
            VMEM((seq,) + block, jnp.bfloat16),
            dma((3, 4, 2)), dma((3, 4, 2)),
            dma((3, 8)), dma((3, 8)),
            dma((2, 8)), dma((2, 8)),
            dma((2, 8)), dma((2, 8)),
            dma((2, 8)), dma((2, 8)),
            dma((2, 8)),
            dma((8,)), dma((8,)),
        ],
        compiler_params=pltpu.CompilerParams(
            collective_id=0, has_side_effects=True, vmem_limit_bytes=EXCHANGE_VMEM
        ),
        name="exchange",
    )(blocks, lengths)


def finish_kernel(
    lens_ref, slots_ref, kv_ref, att_ref, out_ref, kc_ref, vc_ref,
    att, flipped, kv, cut, att_s, in_s, cut_s,
):
    h = lax.axis_index("head")
    seq, tok = kv_ref.shape[1], kv_ref.shape[3]
    steps = seq // 2
    begin, length, end = 0, 0, 0
    for r in range(4):
        mine = slots_ref[0, r] == h
        begin = jnp.where(mine, end, begin)
        length = jnp.where(mine, lens_ref[0, r], length)
        end += lens_ref[0, r]
    first, shift = begin // tok, begin % tok

    def load(t, i):
        blk = jnp.minimum(first + i, seq - 1)
        return pltpu.make_async_copy(kv_ref.at[t, blk], kv.at[t, i], in_s.at[t, i])

    def save(t, i):
        to = (vc_ref, kc_ref)[t]
        return pltpu.make_async_copy(cut.at[t, i], to.at[pl.ds(i * tok, tok)], cut_s.at[t, i])

    take = pltpu.make_async_copy(att_ref, att, att_s.at[0])
    give = pltpu.make_async_copy(flipped, out_ref, att_s.at[1])
    take.start()
    for i in range(steps + 1):
        for t in (V, K):
            load(t, i).start()
    take.wait()
    flipped[...] = att[...].T
    row = lax.broadcasted_iota(jnp.int32, (tok, tok), 0)
    col = lax.broadcasted_iota(jnp.int32, (tok, tok), 1)
    dims = (((1,), (1,)), ((), ()))
    for t in (V, K):
        load(t, 0).wait()
    pending = give
    for i in range(steps):
        kept = row + i * tok < length
        low = jnp.where(kept & (col == row + shift), 1.0, 0.0).astype(jnp.bfloat16)
        high = jnp.where(kept & (col + tok == row + shift), 1.0, 0.0).astype(jnp.bfloat16)
        for t in (V, K):
            load(t, i + 1).wait()
            part = lax.dot_general(low, kv[t, i], dims, preferred_element_type=jnp.float32)
            part += lax.dot_general(high, kv[t, i + 1], dims, preferred_element_type=jnp.float32)
            cut[t, i] = part.astype(jnp.bfloat16)
            pending.start()
            pending = save(t, i)
    pending.start()
    give.wait()
    for i in range(steps):
        for t in (V, K):
            save(t, i).wait()


def finish(lengths, slots, kv, attended):
    _, seq, rows, tok = kv.shape
    wide = attended.shape[0]
    steps = seq // 2
    anywhere = pl.BlockSpec(memory_space=pl.ANY)
    scalars = pl.BlockSpec(memory_space=pltpu.SMEM)
    dma = pltpu.SemaphoreType.DMA
    cache = jax.ShapeDtypeStruct((steps * tok, rows), jnp.bfloat16)
    return pl.pallas_call(
        finish_kernel,
        out_shape=(jax.ShapeDtypeStruct((tok, wide), jnp.bfloat16), cache, cache),
        in_specs=[scalars, scalars, anywhere, anywhere],
        out_specs=(anywhere, anywhere, anywhere),
        scratch_shapes=[
            VMEM((wide, tok), jnp.bfloat16),
            VMEM((tok, wide), jnp.bfloat16),
            VMEM((2, steps + 1, rows, tok), jnp.bfloat16),
            VMEM((2, steps, tok, rows), jnp.bfloat16),
            dma((2,)), dma((2, steps + 1)), dma((2, steps)),
        ],
        compiler_params=pltpu.CompilerParams(vmem_limit_bytes=FINISH_VMEM),
        name="finish",
    )(lengths, slots, kv, attended)


def per_device(queries, new_keys, new_values, lengths, offsets, slot_map):
    tok = queries.shape[1]
    seq = lax.axis_size("seq")
    rates = jnp.power(
        jnp.float32(ROPE_BASE), -2.0 * jnp.arange(HALF, dtype=jnp.float32) / HD
    )
    blocks = rotated_blocks(
        lengths, offsets, queries[0], new_keys[0], new_values[0], rates[:, None]
    )
    kv, attended = exchange(blocks, lengths)
    out, keys, values = finish(
        lengths, slot_map, kv.reshape(2, seq, 4 * HD, tok), attended.reshape(8 * HD, tok)
    )
    return out[None], keys[None, None], values[None, None]


def solution(mesh):
    full = P("rep", "seq", "head")
    row = P("rep", None)
    cache = P("rep", "head", None, "seq")
    return jax.shard_map(
        per_device, mesh=mesh, in_specs=(full, full, full, row, row, row),
        out_specs=(full, cache, cache), check_vma=False,
    )
```

```python
import functools
import math

import jax
import jax.numpy as jnp
from jax import lax
from jax.experimental import pallas as pl
from jax.experimental.pallas import tpu as pltpu
from jax.sharding import PartitionSpec as P

HD = 224
HALF = HD // 2
ROPE_BASE = 10000.0
NEG_FILL = -1e30
MESH = pl.DeviceIdType.MESH
VMEM = pltpu.VMEM
STEPS = (4, 3, -3, 2, -2, 1, -1)
V, K, Q = 0, 1, 2
EXCHANGE_VMEM = 28 << 20
FINISH_VMEM = 28 << 20


def rotate_kernel(lens_ref, offs_ref, v_ref, k_ref, q_ref, rate_ref, out_ref, cos_ref, sin_ref):
    @pl.when(pl.program_id(0) == 0)
    def _():
        tok = cos_ref.shape[-1]
        token = lax.broadcasted_iota(jnp.int32, (1, tok), 1) + lax.axis_index("seq") * tok
        ahead = jnp.full((1, tok), offs_ref[0, 0], jnp.int32)
        end = lens_ref[0, 0]
        for r in range(1, 4):
            ahead = jnp.where(token >= end, offs_ref[0, r] - end, ahead)
            end += lens_ref[0, r]
        angles = rate_ref[...] * (token + ahead).astype(jnp.float32)
        cos_ref[...] = jnp.cos(angles)
        sin_ref[...] = jnp.sin(angles)

    cos, sin = cos_ref[...], sin_ref[...]
    for t, ref in ((V, v_ref), (K, k_ref), (Q, q_ref)):
        flipped = ref[...].T
        for i in range(4):
            if t == V:
                out_ref[t, i, 0] = flipped[i * HD : (i + 1) * HD]
            else:
                a = flipped[i * HD : i * HD + HALF].astype(jnp.float32)
                b = flipped[i * HD + HALF : (i + 1) * HD].astype(jnp.float32)
                out_ref[t, i, 0, :HALF] = (a * cos - b * sin).astype(jnp.bfloat16)
                out_ref[t, i, 0, HALF:] = (b * cos + a * sin).astype(jnp.bfloat16)


def rotated_blocks(lengths, offsets, queries, keys, values, rates):
    tok = queries.shape[0]
    wide = pl.BlockSpec((tok, 4 * HD), lambda e: (0, e))
    scalars = pl.BlockSpec(memory_space=pltpu.SMEM)
    return pl.pallas_call(
        rotate_kernel,
        grid=(2,),
        out_shape=jax.ShapeDtypeStruct((3, 4, 2, HD, tok), jnp.bfloat16),
        in_specs=[
            scalars, scalars, wide, wide, wide, pl.BlockSpec((HALF, 1), lambda e: (0, 0)),
        ],
        out_specs=pl.BlockSpec((3, 4, 1, HD, tok), lambda e: (0, 0, e, 0, 0)),
        scratch_shapes=[VMEM((HALF, tok), jnp.float32), VMEM((HALF, tok), jnp.float32)],
        compiler_params=pltpu.CompilerParams(vmem_limit_bytes=48 << 20),
        name="rotate",
    )(lengths, offsets, values, keys, queries, rates)


def exchange_kernel(
    x_ref, lens_ref, kv_ref, out_ref,
    mid, rec, kn, osend,
    in_s, in_r, z_s, z_r, y_s, y_r, c_s, c_r, f_s, f_r, own_s, o_s, o_r,
):
    s, h, r = lax.axis_index("seq"), lax.axis_index("head"), lax.axis_index("rep")
    tok = rec.shape[-1]
    core, high = h % 2, h // 2
    c1 = high * 2 + (1 - core)
    y1 = (1 - high) * 2 + core
    y2 = (1 - high) * 2 + (1 - core)
    partners = (h, c1, y1, y2)
    o_self = s // 2 == h

    def remote(src, dst, send, recv, seq, head):
        return pltpu.make_async_remote_copy(
            src_ref=src, dst_ref=dst, send_sem=send, recv_sem=recv,
            device_id=(seq, head, r), device_id_type=MESH,
        )

    bar = pltpu.get_barrier_semaphore()
    for p in partners[1:]:
        pl.semaphore_signal(bar, inc=1, device_id=(s, p, r), device_id_type=MESH)
    for d in range(1, 8):
        pl.semaphore_signal(bar, inc=1, device_id=((s + d) % 8, h, r), device_id_type=MESH)
    for e in range(2):
        for p in range(4):
            here = (2 * h + e == s) & (p == h)

            @pl.when(jnp.logical_not(here))
            def _():
                pl.semaphore_signal(bar, inc=1, device_id=(2 * h + e, p, r), device_id_type=MESH)

    @pl.when(o_self)
    def _():
        pl.semaphore_wait(bar, 17)

    @pl.when(jnp.logical_not(o_self))
    def _():
        pl.semaphore_wait(bar, 18)

    def plane(t, rel, e):
        return remote(
            x_ref.at[t, partners[rel], e], mid.at[t, rel, e],
            in_s.at[t, rel, e], in_r.at[t, rel, e], s, partners[rel],
        )

    def plane_own(t, e):
        return pltpu.make_async_copy(x_ref.at[t, h, e], mid.at[t, 0, e], in_r.at[t, 0, e])

    for t in (V, K, Q):
        for e in range(2):
            plane(t, 2, e).start()
            plane(t, 3, e).start()
        for e in range(2):
            plane_own(t, e).start()
            plane(t, 1, e).start()

    def z_place(to):
        hs, e = to // 2, to % 2
        rel = (h % 2 + hs % 2) % 2 + 2 * ((h // 2 + hs // 2) % 2)
        return rel, e

    def z_issue(t):
        def z_send(n, to, rel, e):
            pltpu.make_async_copy(mid.at[t, rel, e], mid.at[t, rel, e], in_r.at[t, rel, e]).wait()
            remote(mid.at[t, rel, e], rec.at[t, s], z_s.at[t, n], z_r.at[t, n], to, h).start()

        for passes in ((0, 1) if t == V else (None,)):
            for n, d in enumerate(STEPS):
                to = (s + d + 8) % 8
                rel, e = z_place(to)
                if passes is None:
                    z_send(n, to, rel, e)
                else:
                    pl.when(rel // 2 == passes)(functools.partial(z_send, n, to, rel, e))
        rel, e = z_place(s)
        pltpu.make_async_copy(mid.at[t, rel, e], mid.at[t, rel, e], in_r.at[t, rel, e]).wait()
        pltpu.make_async_copy(mid.at[t, rel, e], rec.at[t, s], z_r.at[t, 7]).start()

    def z_from(n):
        return s if n == 7 else (s - STEPS[n] + 8) % 8

    def z_wait(t, n):
        blk = z_from(n)
        pltpu.make_async_copy(rec.at[t, blk], rec.at[t, blk], z_r.at[t, n]).wait()
        return blk

    def share(t, n, blk):
        return (
            remote(rec.at[t, blk], kv_ref.at[t, blk, h], y_s.at[t, n], y_r.at[t, n], s, y1),
            remote(rec.at[t, blk], kv_ref.at[t, blk, h], c_s.at[t, n], c_r.at[t, n], s, c1),
            pltpu.make_async_copy(rec.at[t, blk], kv_ref.at[t, blk, h], own_s.at[t, n]),
        )

    def pass_on(t, n):
        blk = z_from(n)
        return remote(
            kv_ref.at[t, blk, y1], kv_ref.at[t, blk, y1], f_s.at[t, n], f_r.at[t, n], s, c1
        )

    def pass_wait(t, n):
        share(t, n, z_from(n))[0].wait_recv()
        pass_on(t, n).start()

    z_issue(V)
    z_issue(K)
    for n in (7, 0, 1, 2, 3, 4, 5, 6):
        blk = z_wait(V, n)
        for copy in share(V, n, blk):
            copy.start()
    z_issue(Q)
    for n in (7, 0, 1, 2, 3, 4, 5, 6):
        blk = z_wait(K, n)
        for copy in share(K, n, blk):
            copy.start()
        kn[blk] = rec[K, blk].T

    key_rel = lax.broadcasted_iota(jnp.int32, (tok, tok), 0)
    query_rel = lax.broadcasted_iota(jnp.int32, (tok, tok), 1)
    rate = math.log2(math.e) / math.sqrt(HD)
    prompt = lens_ref[0, 0]
    token_rel = lax.broadcasted_iota(jnp.int32, (1, tok), 1)

    def attend(blk):
        q = rec[Q, blk]
        token = token_rel + blk * tok
        first = jnp.zeros_like(token)
        end = 0
        for r in range(3):
            end += lens_ref[0, r]
            first = jnp.where(token >= end, end, first)

        def scores(j):
            raw = jnp.dot(kn[j], q, preferred_element_type=jnp.float32)
            place = key_rel + j * tok
            return raw, (place < prompt) | (place >= first)

        raw, seen = scores(blk)
        sc = jnp.where(seen & (key_rel <= query_rel), raw, NEG_FILL)
        best = jnp.max(sc, axis=0, keepdims=True)
        w = jnp.exp2((sc - best) * rate)
        total = jnp.sum(w, axis=0, keepdims=True)
        acc = jnp.dot(rec[V, blk], w.astype(jnp.bfloat16), preferred_element_type=jnp.float32)

        def step(j, state):
            best, total, acc = state
            raw, seen = scores(j)
            sc = jnp.where(seen, raw, NEG_FILL)
            new = jnp.maximum(best, jnp.max(sc, axis=0, keepdims=True))
            keep = jnp.exp2((best - new) * rate)
            w = jnp.exp2((sc - new) * rate)
            total = total * keep + jnp.sum(w, axis=0, keepdims=True)
            acc = acc * keep + jnp.dot(
                rec[V, j], w.astype(jnp.bfloat16), preferred_element_type=jnp.float32
            )
            return new, total, acc

        best, total, acc = lax.fori_loop(0, blk, step, (best, total, acc))
        osend[blk] = (acc / total).astype(jnp.bfloat16)

    mine = (s % 2) * 4 + h

    def give(blk, n):
        return remote(osend.at[blk], out_ref.at[mine], o_s.at[n], o_r.at[mine], blk, s // 2)

    def give_own():
        return pltpu.make_async_copy(osend.at[s], out_ref.at[mine], o_r.at[mine])

    for n in (7, 0, 1, 2, 3, 4, 5, 6):
        blk = z_wait(Q, n)
        attend(blk)
        if n < 7:
            give(blk, n).start()
        else:

            @pl.when(o_self)
            def _():
                give_own().start()

            @pl.when(jnp.logical_not(o_self))
            def _():
                give(blk, 7).start()

        pass_wait(V, n)
    for n in (7, 0, 1, 2, 3, 4, 5, 6):
        pass_wait(K, n)

    for j in range(8):
        pltpu.make_async_copy(out_ref.at[j], out_ref.at[j], o_r.at[j]).wait()
    for t in (V, K):
        for n in range(8):
            yc, cc, oc = share(t, n, z_from(n))
            oc.wait()
            yc.wait_send()
            cc.wait()
            pass_on(t, n).wait()
    for t in (V, K, Q):
        for e in range(2):
            for rel in (1, 2, 3):
                plane(t, rel, e).wait_send()
        for n in range(7):
            remote(rec.at[t, s], rec.at[t, s], z_s.at[t, n], z_r.at[t, n], s, c1).wait_send()
    for n in range(7):
        give(z_from(n), n).wait_send()

    @pl.when(jnp.logical_not(o_self))
    def _():
        give(s, 7).wait_send()


def exchange(blocks, lengths):
    tok = blocks.shape[-1]
    seq = 2048 // tok
    dma = pltpu.SemaphoreType.DMA
    block = (HD, tok)
    return pl.pallas_call(
        exchange_kernel,
        out_shape=(
            jax.ShapeDtypeStruct((2, seq, 4) + block, jnp.bfloat16),
            jax.ShapeDtypeStruct((8,) + block, jnp.bfloat16),
        ),
        in_specs=[
            pl.BlockSpec(memory_space=pl.ANY),
            pl.BlockSpec(memory_space=pltpu.SMEM),
        ],
        out_specs=(pl.BlockSpec(memory_space=pl.ANY), pl.BlockSpec(memory_space=pl.ANY)),
        scratch_shapes=[
            VMEM((3, 4, 2) + block, jnp.bfloat16),
            VMEM((3, seq) + block, jnp.bfloat16),
            VMEM((seq, tok, HD), jnp.bfloat16),
            VMEM((seq,) + block, jnp.bfloat16),
            dma((3, 4, 2)), dma((3, 4, 2)),
            dma((3, 8)), dma((3, 8)),
            dma((2, 8)), dma((2, 8)),
            dma((2, 8)), dma((2, 8)),
            dma((2, 8)), dma((2, 8)),
            dma((2, 8)),
            dma((8,)), dma((8,)),
        ],
        compiler_params=pltpu.CompilerParams(
            collective_id=0, has_side_effects=True, vmem_limit_bytes=EXCHANGE_VMEM
        ),
        name="exchange",
    )(blocks, lengths)


def finish_kernel(
    lens_ref, slots_ref, kv_ref, att_ref, out_ref, kc_ref, vc_ref, flipped, cut, out_s, cut_s,
):
    h = lax.axis_index("head")
    seq, tok = kv_ref.shape[1], kv_ref.shape[3]
    steps = seq // 2
    begin, length, end = 0, 0, 0
    for r in range(4):
        mine = slots_ref[0, r] == h
        begin = jnp.where(mine, end, begin)
        length = jnp.where(mine, lens_ref[0, r], length)
        end += lens_ref[0, r]
    first, shift = begin // tok, begin % tok

    def block(t, i):
        return kv_ref[t, jnp.minimum(first + i, seq - 1)]

    def save(t, i):
        to = (vc_ref, kc_ref)[t]
        return pltpu.make_async_copy(cut.at[t, i], to.at[pl.ds(i * tok, tok)], cut_s.at[t, i])

    give = pltpu.make_async_copy(flipped, out_ref, out_s)
    flipped[...] = att_ref[...].T
    row = lax.broadcasted_iota(jnp.int32, (tok, tok), 0)
    col = lax.broadcasted_iota(jnp.int32, (tok, tok), 1)
    dims = (((1,), (1,)), ((), ()))
    pending = give
    for i in range(steps):
        kept = row + i * tok < length
        low = jnp.where(kept & (col == row + shift), 1.0, 0.0).astype(jnp.bfloat16)
        high = jnp.where(kept & (col + tok == row + shift), 1.0, 0.0).astype(jnp.bfloat16)
        for t in (V, K):
            part = lax.dot_general(low, block(t, i), dims, preferred_element_type=jnp.float32)
            part += lax.dot_general(high, block(t, i + 1), dims, preferred_element_type=jnp.float32)
            cut[t, i] = part.astype(jnp.bfloat16)
            pending.start()
            pending = save(t, i)
    pending.start()
    give.wait()
    for i in range(steps):
        for t in (V, K):
            save(t, i).wait()


def finish(lengths, slots, kv, attended):
    _, seq, rows, tok = kv.shape
    wide = attended.shape[0]
    steps = seq // 2
    anywhere = pl.BlockSpec(memory_space=pl.ANY)
    scalars = pl.BlockSpec(memory_space=pltpu.SMEM)
    dma = pltpu.SemaphoreType.DMA
    cache = jax.ShapeDtypeStruct((steps * tok, rows), jnp.bfloat16)
    return pl.pallas_call(
        finish_kernel,
        out_shape=(jax.ShapeDtypeStruct((tok, wide), jnp.bfloat16), cache, cache),
        in_specs=[
            scalars, scalars, pl.BlockSpec(memory_space=VMEM), pl.BlockSpec(memory_space=VMEM),
        ],
        out_specs=(anywhere, anywhere, anywhere),
        scratch_shapes=[
            VMEM((tok, wide), jnp.bfloat16),
            VMEM((2, steps, tok, rows), jnp.bfloat16),
            dma, dma((2, steps)),
        ],
        compiler_params=pltpu.CompilerParams(vmem_limit_bytes=FINISH_VMEM),
        name="finish",
    )(lengths, slots, kv, attended)


def per_device(queries, new_keys, new_values, lengths, offsets, slot_map):
    tok = queries.shape[1]
    seq = lax.axis_size("seq")
    rates = jnp.power(
        jnp.float32(ROPE_BASE), -2.0 * jnp.arange(HALF, dtype=jnp.float32) / HD
    )
    blocks = rotated_blocks(
        lengths, offsets, queries[0], new_keys[0], new_values[0], rates[:, None]
    )
    kv, attended = exchange(blocks, lengths)
    out, keys, values = finish(
        lengths, slot_map, kv.reshape(2, seq, 4 * HD, tok), attended.reshape(8 * HD, tok)
    )
    return out[None], keys[None, None], values[None, None]


def solution(mesh):
    full = P("rep", "seq", "head")
    row = P("rep", None)
    cache = P("rep", "head", None, "seq")
    return jax.shard_map(
        per_device, mesh=mesh, in_specs=(full, full, full, row, row, row),
        out_specs=(full, cache, cache), check_vma=False,
    )
```

```python
import functools
import math

import jax
import jax.numpy as jnp
from jax import lax
from jax.experimental import pallas as pl
from jax.experimental.pallas import tpu as pltpu
from jax.sharding import PartitionSpec as P

HD = 224
HALF = HD // 2
ROPE_BASE = 10000.0
NEG_FILL = -1e30
MESH = pl.DeviceIdType.MESH
VMEM = pltpu.VMEM
STEPS = (4, 3, -3, 2, -2, 1, -1)
V, K, Q = 0, 1, 2
EXCHANGE_VMEM = 28 << 20
FINISH_VMEM = 28 << 20


def rotate_kernel(lens_ref, offs_ref, v_ref, k_ref, q_ref, rate_ref, out_ref, cos_ref, sin_ref):
    @pl.when(pl.program_id(0) == 0)
    def _():
        tok = cos_ref.shape[-1]
        token = lax.broadcasted_iota(jnp.int32, (1, tok), 1) + lax.axis_index("seq") * tok
        ahead = jnp.full((1, tok), offs_ref[0, 0], jnp.int32)
        end = lens_ref[0, 0]
        for r in range(1, 4):
            ahead = jnp.where(token >= end, offs_ref[0, r] - end, ahead)
            end += lens_ref[0, r]
        angles = rate_ref[...] * (token + ahead).astype(jnp.float32)
        cos_ref[...] = jnp.cos(angles)
        sin_ref[...] = jnp.sin(angles)

    cos, sin = cos_ref[...], sin_ref[...]
    for t, ref in ((V, v_ref), (K, k_ref), (Q, q_ref)):
        flipped = ref[...].T
        for i in range(4):
            if t == V:
                out_ref[t, i, 0] = flipped[i * HD : (i + 1) * HD]
            else:
                a = flipped[i * HD : i * HD + HALF].astype(jnp.float32)
                b = flipped[i * HD + HALF : (i + 1) * HD].astype(jnp.float32)
                out_ref[t, i, 0, :HALF] = (a * cos - b * sin).astype(jnp.bfloat16)
                out_ref[t, i, 0, HALF:] = (b * cos + a * sin).astype(jnp.bfloat16)


def rotated_blocks(lengths, offsets, queries, keys, values, rates):
    tok = queries.shape[0]
    wide = pl.BlockSpec((tok, 4 * HD), lambda e: (0, e))
    scalars = pl.BlockSpec(memory_space=pltpu.SMEM)
    return pl.pallas_call(
        rotate_kernel,
        grid=(2,),
        out_shape=jax.ShapeDtypeStruct((3, 4, 2, HD, tok), jnp.bfloat16),
        in_specs=[
            scalars, scalars, wide, wide, wide, pl.BlockSpec((HALF, 1), lambda e: (0, 0)),
        ],
        out_specs=pl.BlockSpec((3, 4, 1, HD, tok), lambda e: (0, 0, e, 0, 0)),
        scratch_shapes=[VMEM((HALF, tok), jnp.float32), VMEM((HALF, tok), jnp.float32)],
        compiler_params=pltpu.CompilerParams(vmem_limit_bytes=48 << 20),
        name="rotate",
    )(lengths, offsets, values, keys, queries, rates)


def exchange_kernel(
    x_ref, lens_ref, kv_ref, out_ref,
    mid, rec, kn, osend,
    in_s, in_r, z_s, z_r, y_s, y_r, c_s, c_r, f_s, f_r, own_s, o_s, o_r,
):
    s, h, r = lax.axis_index("seq"), lax.axis_index("head"), lax.axis_index("rep")
    tok = rec.shape[-1]
    core, high = h % 2, h // 2
    c1 = high * 2 + (1 - core)
    y1 = (1 - high) * 2 + core
    y2 = (1 - high) * 2 + (1 - core)
    partners = (h, c1, y1, y2)
    o_self = s // 2 == h

    def remote(src, dst, send, recv, seq, head):
        return pltpu.make_async_remote_copy(
            src_ref=src, dst_ref=dst, send_sem=send, recv_sem=recv,
            device_id=(seq, head, r), device_id_type=MESH,
        )

    bar = pltpu.get_barrier_semaphore()
    for p in partners[1:]:
        pl.semaphore_signal(bar, inc=1, device_id=(s, p, r), device_id_type=MESH)
    for d in range(1, 8):
        pl.semaphore_signal(bar, inc=1, device_id=((s + d) % 8, h, r), device_id_type=MESH)
    for e in range(2):
        for p in range(4):
            here = (2 * h + e == s) & (p == h)

            @pl.when(jnp.logical_not(here))
            def _():
                pl.semaphore_signal(bar, inc=1, device_id=(2 * h + e, p, r), device_id_type=MESH)

    @pl.when(o_self)
    def _():
        pl.semaphore_wait(bar, 17)

    @pl.when(jnp.logical_not(o_self))
    def _():
        pl.semaphore_wait(bar, 18)

    def plane(t, rel, e):
        return remote(
            x_ref.at[t, partners[rel], e], mid.at[t, rel, e],
            in_s.at[t, rel, e], in_r.at[t, rel, e], s, partners[rel],
        )

    def plane_own(t, e):
        return pltpu.make_async_copy(x_ref.at[t, h, e], mid.at[t, 0, e], in_r.at[t, 0, e])

    for t in (V, K, Q):
        for e in range(2):
            plane(t, 2, e).start()
            plane(t, 3, e).start()
        for e in range(2):
            plane_own(t, e).start()
            plane(t, 1, e).start()

    def z_place(to):
        hs, e = to // 2, to % 2
        rel = (h % 2 + hs % 2) % 2 + 2 * ((h // 2 + hs // 2) % 2)
        return rel, e

    def z_issue(t):
        for n, d in enumerate(STEPS):
            to = (s + d + 8) % 8
            rel, e = z_place(to)
            pltpu.make_async_copy(mid.at[t, rel, e], mid.at[t, rel, e], in_r.at[t, rel, e]).wait()
            remote(mid.at[t, rel, e], rec.at[t, s], z_s.at[t, n], z_r.at[t, n], to, h).start()
        rel, e = z_place(s)
        pltpu.make_async_copy(mid.at[t, rel, e], mid.at[t, rel, e], in_r.at[t, rel, e]).wait()
        pltpu.make_async_copy(mid.at[t, rel, e], rec.at[t, s], z_r.at[t, 7]).start()

    def z_from(n):
        return s if n == 7 else (s - STEPS[n] + 8) % 8

    def z_wait(t, n):
        blk = z_from(n)
        pltpu.make_async_copy(rec.at[t, blk], rec.at[t, blk], z_r.at[t, n]).wait()
        return blk

    def share(t, n, blk):
        return (
            remote(rec.at[t, blk], kv_ref.at[t, blk, h], y_s.at[t, n], y_r.at[t, n], s, y1),
            remote(rec.at[t, blk], kv_ref.at[t, blk, h], c_s.at[t, n], c_r.at[t, n], s, c1),
            pltpu.make_async_copy(rec.at[t, blk], kv_ref.at[t, blk, h], own_s.at[t, n]),
        )

    def pass_on(t, n):
        blk = z_from(n)
        return remote(
            kv_ref.at[t, blk, y1], kv_ref.at[t, blk, y1], f_s.at[t, n], f_r.at[t, n], s, c1
        )

    def pass_wait(t, n):
        share(t, n, z_from(n))[0].wait_recv()
        pass_on(t, n).start()

    z_issue(V)
    z_issue(K)
    for n in (7, 0, 1, 2, 3, 4, 5, 6):
        blk = z_wait(V, n)
        for copy in share(V, n, blk):
            copy.start()
    z_issue(Q)
    for n in (7, 0, 1, 2, 3, 4, 5, 6):
        blk = z_wait(K, n)
        for copy in share(K, n, blk):
            copy.start()
        kn[blk] = rec[K, blk].T

    key_rel = lax.broadcasted_iota(jnp.int32, (tok, tok), 0)
    query_rel = lax.broadcasted_iota(jnp.int32, (tok, tok), 1)
    rate = math.log2(math.e) / math.sqrt(HD)
    prompt = lens_ref[0, 0]
    token_rel = lax.broadcasted_iota(jnp.int32, (1, tok), 1)

    def attend(blk):
        q = rec[Q, blk]
        token = token_rel + blk * tok
        first = jnp.zeros_like(token)
        end = 0
        for r in range(3):
            end += lens_ref[0, r]
            first = jnp.where(token >= end, end, first)

        def scores(j):
            raw = jnp.dot(kn[j], q, preferred_element_type=jnp.float32)
            place = key_rel + j * tok
            return raw, (place < prompt) | (place >= first)

        raw, seen = scores(blk)
        sc = jnp.where(seen & (key_rel <= query_rel), raw, NEG_FILL)
        best = jnp.max(sc, axis=0, keepdims=True)
        w = jnp.exp2((sc - best) * rate)
        total = jnp.sum(w, axis=0, keepdims=True)
        acc = jnp.dot(rec[V, blk], w.astype(jnp.bfloat16), preferred_element_type=jnp.float32)

        def step(j, state):
            best, total, acc = state
            raw, seen = scores(j)
            sc = jnp.where(seen, raw, NEG_FILL)
            new = jnp.maximum(best, jnp.max(sc, axis=0, keepdims=True))
            keep = jnp.exp2((best - new) * rate)
            w = jnp.exp2((sc - new) * rate)
            total = total * keep + jnp.sum(w, axis=0, keepdims=True)
            acc = acc * keep + jnp.dot(
                rec[V, j], w.astype(jnp.bfloat16), preferred_element_type=jnp.float32
            )
            return new, total, acc

        best, total, acc = lax.fori_loop(0, blk, step, (best, total, acc))
        osend[blk] = (acc / total).astype(jnp.bfloat16)

    mine = (s % 2) * 4 + h

    def give(blk, n):
        return remote(osend.at[blk], out_ref.at[mine], o_s.at[n], o_r.at[mine], blk, s // 2)

    def give_own():
        return pltpu.make_async_copy(osend.at[s], out_ref.at[mine], o_r.at[mine])

    for n in range(8):
        blk = z_wait(Q, n)
        attend(blk)
        if n < 7:
            give(blk, n).start()
        else:

            @pl.when(o_self)
            def _():
                give_own().start()

            @pl.when(jnp.logical_not(o_self))
            def _():
                give(blk, 7).start()

        pass_wait(V, (7, 0, 1, 2, 3, 4, 5, 6)[n])
    for n in (7, 0, 1, 2, 3, 4, 5, 6):
        pass_wait(K, n)

    for j in range(8):
        pltpu.make_async_copy(out_ref.at[j], out_ref.at[j], o_r.at[j]).wait()
    for t in (V, K):
        for n in range(8):
            yc, cc, oc = share(t, n, z_from(n))
            oc.wait()
            yc.wait_send()
            cc.wait()
            pass_on(t, n).wait()
    for t in (V, K, Q):
        for e in range(2):
            for rel in (1, 2, 3):
                plane(t, rel, e).wait_send()
        for n in range(7):
            remote(rec.at[t, s], rec.at[t, s], z_s.at[t, n], z_r.at[t, n], s, c1).wait_send()
    for n in range(7):
        give(z_from(n), n).wait_send()

    @pl.when(jnp.logical_not(o_self))
    def _():
        give(s, 7).wait_send()


def exchange(blocks, lengths):
    tok = blocks.shape[-1]
    seq = 2048 // tok
    dma = pltpu.SemaphoreType.DMA
    block = (HD, tok)
    return pl.pallas_call(
        exchange_kernel,
        out_shape=(
            jax.ShapeDtypeStruct((2, seq, 4) + block, jnp.bfloat16),
            jax.ShapeDtypeStruct((8,) + block, jnp.bfloat16),
        ),
        in_specs=[
            pl.BlockSpec(memory_space=pl.ANY),
            pl.BlockSpec(memory_space=pltpu.SMEM),
        ],
        out_specs=(pl.BlockSpec(memory_space=pl.ANY), pl.BlockSpec(memory_space=pl.ANY)),
        scratch_shapes=[
            VMEM((3, 4, 2) + block, jnp.bfloat16),
            VMEM((3, seq) + block, jnp.bfloat16),
            VMEM((seq, tok, HD), jnp.bfloat16),
            VMEM((seq,) + block, jnp.bfloat16),
            dma((3, 4, 2)), dma((3, 4, 2)),
            dma((3, 8)), dma((3, 8)),
            dma((2, 8)), dma((2, 8)),
            dma((2, 8)), dma((2, 8)),
            dma((2, 8)), dma((2, 8)),
            dma((2, 8)),
            dma((8,)), dma((8,)),
        ],
        compiler_params=pltpu.CompilerParams(
            collective_id=0, has_side_effects=True, vmem_limit_bytes=EXCHANGE_VMEM
        ),
        name="exchange",
    )(blocks, lengths)


def finish_kernel(
    lens_ref, slots_ref, kv_ref, att_ref, out_ref, kc_ref, vc_ref, flipped, cut, out_s, cut_s,
):
    h = lax.axis_index("head")
    seq, tok = kv_ref.shape[1], kv_ref.shape[3]
    steps = seq // 2
    begin, length, end = 0, 0, 0
    for r in range(4):
        mine = slots_ref[0, r] == h
        begin = jnp.where(mine, end, begin)
        length = jnp.where(mine, lens_ref[0, r], length)
        end += lens_ref[0, r]
    first, shift = begin // tok, begin % tok

    def block(t, i):
        return kv_ref[t, jnp.minimum(first + i, seq - 1)]

    def save(t, i):
        to = (vc_ref, kc_ref)[t]
        return pltpu.make_async_copy(cut.at[t, i], to.at[pl.ds(i * tok, tok)], cut_s.at[t, i])

    give = pltpu.make_async_copy(flipped, out_ref, out_s)
    flipped[...] = att_ref[...].T
    row = lax.broadcasted_iota(jnp.int32, (tok, tok), 0)
    col = lax.broadcasted_iota(jnp.int32, (tok, tok), 1)
    dims = (((1,), (1,)), ((), ()))
    pending = give
    for i in range(steps):
        kept = row + i * tok < length
        low = jnp.where(kept & (col == row + shift), 1.0, 0.0).astype(jnp.bfloat16)
        high = jnp.where(kept & (col + tok == row + shift), 1.0, 0.0).astype(jnp.bfloat16)
        for t in (V, K):
            part = lax.dot_general(low, block(t, i), dims, preferred_element_type=jnp.float32)
            part += lax.dot_general(high, block(t, i + 1), dims, preferred_element_type=jnp.float32)
            cut[t, i] = part.astype(jnp.bfloat16)
            pending.start()
            pending = save(t, i)
    pending.start()
    give.wait()
    for i in range(steps):
        for t in (V, K):
            save(t, i).wait()


def finish(lengths, slots, kv, attended):
    _, seq, rows, tok = kv.shape
    wide = attended.shape[0]
    steps = seq // 2
    anywhere = pl.BlockSpec(memory_space=pl.ANY)
    scalars = pl.BlockSpec(memory_space=pltpu.SMEM)
    dma = pltpu.SemaphoreType.DMA
    cache = jax.ShapeDtypeStruct((steps * tok, rows), jnp.bfloat16)
    return pl.pallas_call(
        finish_kernel,
        out_shape=(jax.ShapeDtypeStruct((tok, wide), jnp.bfloat16), cache, cache),
        in_specs=[
            scalars, scalars, pl.BlockSpec(memory_space=VMEM), pl.BlockSpec(memory_space=VMEM),
        ],
        out_specs=(anywhere, anywhere, anywhere),
        scratch_shapes=[
            VMEM((tok, wide), jnp.bfloat16),
            VMEM((2, steps, tok, rows), jnp.bfloat16),
            dma, dma((2, steps)),
        ],
        compiler_params=pltpu.CompilerParams(vmem_limit_bytes=FINISH_VMEM),
        name="finish",
    )(lengths, slots, kv, attended)


def per_device(queries, new_keys, new_values, lengths, offsets, slot_map):
    tok = queries.shape[1]
    seq = lax.axis_size("seq")
    rates = jnp.power(
        jnp.float32(ROPE_BASE), -2.0 * jnp.arange(HALF, dtype=jnp.float32) / HD
    )
    blocks = rotated_blocks(
        lengths, offsets, queries[0], new_keys[0], new_values[0], rates[:, None]
    )
    kv, attended = exchange(blocks, lengths)
    out, keys, values = finish(
        lengths, slot_map, kv.reshape(2, seq, 4 * HD, tok), attended.reshape(8 * HD, tok)
    )
    return out[None], keys[None, None], values[None, None]


def solution(mesh):
    full = P("rep", "seq", "head")
    row = P("rep", None)
    cache = P("rep", "head", None, "seq")
    return jax.shard_map(
        per_device, mesh=mesh, in_specs=(full, full, full, row, row, row),
        out_specs=(full, cache, cache), check_vma=False,
    )
```
